512 devices in a mesh: mp: 64 (over x, z), replica: 8 (over y, core).
Axes of the slice: x: 4, y: 4, z: 16, core: 2. Of those that a mesh axis runs over, the one named last changes fastest.
Arguments:
- pooled_grads: bfloat16 [64, 8, 128, 64, 128], P('mp', 'replica'), may hold values from -0.119628906 to 0.119628906
- table: float32 [64, 512, 128], P('mp'), may hold values from -3 to 3
- state: float32 [64, 512], P('mp'), may hold values from 0.2 to 5
- tile_mult: bfloat16 [64, 8, 64, 128, 128], P('mp', 'replica'), may hold values from 0 to 3, as said below
- tile_rows: int32 [64, 8, 64], P('mp', 'replica'), may hold values from 0 to 3
Outputs:
- new_table: float32 [64, 512, 128], P('mp')
- new_state: float32 [64, 512], P('mp')
The draws below stay inside these ranges and needn't reach their ends.
Inputs may be any that keep to these rules, and one draw needn't show every extreme that they name: tile_mult holds whole numbers.
All inputs are finite; a program needn't handle non-finite values.
Results may differ from the reference program's by a relative error of at most 0.0003.
Values may be sent and summed in bfloat16 or wider, within the bound.
No kernel may reach another device: no remote copies, remote signals or barrier semaphores. Data moves between devices by JAX's collectives and lax.ppermute only.
A program may use at most 64 MiB of HBM per device.

```python
import math
import jax
import jax.numpy as jnp
import numpy as np
from jax import lax

EMB = 128
BLOCK = 128
S_DEV = 128
ROWS = 512
TABLES = 64
SBLOCKS = 64
RBLOCKS = 4
N_MP = 64
N_REPLICA = 8


def draw_tile_mult(key, part):
    shape_all = (TABLES, N_REPLICA, SBLOCKS, BLOCK, BLOCK)
    uniform_draw = jax.random.uniform(jax.random.fold_in(key, 7), shape_all, jnp.float32, 0.0, 1.0)
    values = jnp.floor(4.0 * uniform_draw)
    values = jnp.clip(values, 0.0, 3.0)
    return values.astype(jnp.bfloat16)


def touch_ends(entries, rng, least, largest):
    spot = [jax.random.randint(jax.random.fold_in(rng, axis), (), 0, length) for axis, length in enumerate(entries.shape)]
    main_axis = entries.shape.index(max(entries.shape))
    beside = spot[:main_axis] + [(spot[main_axis] + 1) % entries.shape[main_axis]] + spot[main_axis + 1:]
    return entries.at[tuple(spot)].set(least).at[tuple(beside)].set(largest)


def block_scale(rng, extent, shards, low, high):
    gain, own = 1.0, jax.random.fold_in(rng, 6)
    for axis_at, parts in shards:
        heights = jnp.exp(jax.random.uniform(jax.random.fold_in(own, axis_at), (parts,), jnp.float32, low / len(shards), high / len(shards)))
        gain = gain * jnp.repeat(heights, extent[axis_at] // parts).reshape([-1 if axis == axis_at else 1 for axis in range(len(extent))])
    return gain


def cumulative_ranks(amount, slope):
    portions = [(1 << 20) // math.isqrt(rank ** slope) + 1 for rank in range(1, amount + 1)]
    scale = 1 + sum(portions) // (1 << 30)
    return np.cumsum(np.array([max(1, weight // scale) for weight in portions]))


def skewed_ids(key, dims, amount, slope):
    listing = cumulative_ranks(amount, slope)
    lot = jax.random.randint(jax.random.fold_in(key, 1), dims, 0, int(listing[amount - 1]))
    rank = jnp.searchsorted(jnp.asarray(listing, jnp.int32), lot, side="right")
    return jax.random.permutation(jax.random.fold_in(key, 2), amount)[rank].astype(jnp.int32)


def bell_draw(key, extent, width, limit, shards=(), kind=jnp.bfloat16):
    drawn = width * jax.random.normal(key, extent, jnp.float32)
    if shards:
        drawn = drawn * block_scale(key, extent, shards, -0.22, 0.18)
    return jnp.clip(drawn, -limit, limit).astype(kind)


def setup_inputs(seed: int = 0) -> dict:
    splits = jax.random.split(jax.random.key(seed), 6)
    pooled_grads = bell_draw(splits[0], (N_MP, N_REPLICA, S_DEV, TABLES, EMB), 0.02, 0.119628906, ((0, 64), (1, 8)))
    table = bell_draw(splits[1], (TABLES, ROWS, EMB), 0.5, 3.0, ((0, 64),), jnp.float32)
    state = jnp.clip(jnp.exp(math.log(5.0) - 3.218876 * jax.random.uniform(splits[2], (TABLES, ROWS), jnp.float32) ** block_scale(splits[2], (TABLES, ROWS), ((0, 64),), -0.2, 0.2)), 0.2, 5.0)
    tile_mult = draw_tile_mult(jax.random.fold_in(splits[5], 71), 0)
    tile_rows = touch_ends(skewed_ids(splits[4], (TABLES, N_REPLICA, SBLOCKS), RBLOCKS, 2), jax.random.fold_in(splits[4], 3), 0, RBLOCKS - 1).astype(jnp.int32)
    return {"pooled_grads": pooled_grads, "table": table, "state": state, "tile_mult": tile_mult, "tile_rows": tile_rows}


LEARN_RATE = 0.5
EPSILON = 1e-06

def one_table(packed):
    grads_f, mult_f, rowsb_f = packed
    per_group = jnp.transpose(grads_f, (1, 0, 2, 3)).reshape(N_REPLICA, SBLOCKS, BLOCK, EMB)
    contrib = jnp.einsum('ktsr,ktse->ktre', mult_f.astype(jnp.float32), per_group.astype(jnp.float32), precision=lax.Precision.HIGHEST)
    onehot = (rowsb_f[..., None] == jnp.arange(RBLOCKS, dtype=jnp.int32)[None, None, :]).astype(jnp.float32)
    summed = jnp.einsum('ktb,ktre->bre', onehot, contrib, precision=lax.Precision.HIGHEST)
    return summed.reshape(ROWS, EMB)

def reference(pooled_grads, table, state, tile_mult, tile_rows):
    by_table = jnp.moveaxis(pooled_grads, 3, 0)
    row_grad = lax.map(one_table, (by_table, tile_mult, tile_rows))
    new_state = state + lax.optimization_barrier(jnp.mean(row_grad * row_grad, axis=-1))
    new_table = table - LEARN_RATE * row_grad / (jnp.sqrt(new_state)[..., None] + EPSILON)
    return (new_table, new_state)
```

```python
import jax
import jax.numpy as jnp
from jax import lax
from jax.experimental import pallas as pl
from jax.experimental.pallas import tpu as pltpu
from jax.sharding import PartitionSpec as P

LEARN_RATE = 0.5
EPSILON = 1e-06


def accumulate_kernel(rows_ref, mult_ref, grads_ref, out_ref):
    tiles, block, _ = mult_ref.shape
    out_ref[...] = jnp.zeros(out_ref.shape, out_ref.dtype)

    def one_tile(t, carry):
        contrib = lax.dot_general(
            mult_ref[t], grads_ref[t], (((0,), (0,)), ((), ())), preferred_element_type=jnp.float32
        )
        out_ref[rows_ref[t]] += contrib
        return carry

    lax.fori_loop(0, tiles, one_tile, 0, unroll=8)


def accumulate(row_ids, mult, grads, row_blocks):
    _, block, width = grads.shape
    vmem = pl.BlockSpec(memory_space=pltpu.VMEM)
    return pl.pallas_call(
        accumulate_kernel,
        out_shape=jax.ShapeDtypeStruct((row_blocks, block, width), jnp.float32),
        in_specs=[pl.BlockSpec(memory_space=pltpu.SMEM), vmem, vmem],
        out_specs=vmem,
        name="accumulate",
    )(row_ids, mult, grads)


def adagrad(weights_in, accum_in, gradient):
    accum_out = accum_in + jnp.mean(gradient * gradient, axis=-1)
    weights_out = weights_in - LEARN_RATE * gradient / (jnp.sqrt(accum_out)[..., None] + EPSILON)
    return (weights_out, accum_out)


def on_device(pooled_grads, table, state, tile_mult, tile_rows):
    weights_in = table[0]
    accum_in = state[0]
    mult = tile_mult[0, 0]
    rows, width = weights_in.shape
    row_blocks = rows // mult.shape[-1]
    replicas = lax.axis_size("replica")

    by_table = jnp.transpose(pooled_grads[0, 0], (1, 0, 2))
    received = lax.all_to_all(by_table, "mp", split_axis=0, concat_axis=0, tiled=True)
    partial_grad = accumulate(tile_rows[0, 0], mult, received, row_blocks)

    shares = partial_grad.reshape(replicas, rows // replicas, width)
    shares = lax.all_to_all(shares, "replica", split_axis=0, concat_axis=0, tiled=True)
    own = jnp.sum(shares, axis=0)
    copies = jnp.broadcast_to(own[None], (replicas,) + own.shape)
    total_grad = lax.all_to_all(copies, "replica", split_axis=0, concat_axis=0, tiled=True)

    weights_out, accum_out = adagrad(weights_in, accum_in, total_grad.reshape(rows, width))
    return (weights_out[None], accum_out[None])


def solution(mesh):
    placed = (
        P("mp", "replica", None, None, None),
        P("mp", None, None),
        P("mp", None),
        P("mp", "replica", None, None, None),
        P("mp", "replica", None),
    )
    return jax.shard_map(
        on_device,
        mesh=mesh,
        in_specs=placed,
        out_specs=(P("mp", None, None), P("mp", None)),
        check_vma=False,
    )
```

```python
import jax
import jax.numpy as jnp
from jax import lax
from jax.experimental import pallas as pl
from jax.experimental.pallas import tpu as pltpu
from jax.sharding import PartitionSpec as P

LEARN_RATE = 0.5
EPSILON = 1e-06


STEPS = 2


def accumulate_kernel(rows_ref, mult_ref, grads_ref, out_ref):
    step = pl.program_id(0)
    tiles = mult_ref.shape[0]

    @pl.when(step == 0)
    def _():
        out_ref[...] = jnp.zeros(out_ref.shape, out_ref.dtype)

    for t in range(tiles):
        contrib = lax.dot_general(
            mult_ref[t], grads_ref[t], (((0,), (0,)), ((), ())), preferred_element_type=jnp.float32
        )
        out_ref[rows_ref[step * tiles + t]] += contrib


def accumulate(row_ids, mult, grads, row_blocks):
    tiles, block, width = grads.shape
    tile_spec = pl.BlockSpec((tiles // STEPS, block, width), lambda i: (i, 0, 0))
    mult_spec = pl.BlockSpec((tiles // STEPS, block, block), lambda i: (i, 0, 0))
    return pl.pallas_call(
        accumulate_kernel,
        grid=(STEPS,),
        out_shape=jax.ShapeDtypeStruct((row_blocks, block, width), jnp.float32),
        in_specs=[pl.BlockSpec(memory_space=pltpu.SMEM), mult_spec, tile_spec],
        out_specs=pl.BlockSpec((row_blocks, block, width), lambda i: (0, 0, 0)),
        compiler_params=pltpu.CompilerParams(vmem_limit_bytes=16 << 20),
        name="accumulate",
    )(row_ids, mult, grads)


CORES = 2


def sum_over_replicas(partial_grad):
    rows, width = partial_grad.shape
    replicas = lax.axis_size("replica")
    chips = replicas // CORES
    core = lax.axis_index("replica") % CORES
    swap = [(i, i ^ 1) for i in range(replicas)]
    same_core = [[chip * CORES + c for chip in range(chips)] for c in range(CORES)]

    chip_sum = partial_grad + lax.ppermute(partial_grad, "replica", swap)
    half = lax.dynamic_index_in_dim(
        chip_sum.reshape(CORES, rows // CORES, width), core, 0, keepdims=False
    )
    copies = jnp.broadcast_to(half[None], (chips,) + half.shape)
    shares = lax.all_to_all(
        copies, "replica", split_axis=0, concat_axis=0, axis_index_groups=same_core, tiled=True
    )
    own = jnp.sum(shares, axis=0)
    other = lax.ppermute(own, "replica", swap)
    first = core == 0
    return jnp.concatenate([jnp.where(first, own, other), jnp.where(first, other, own)])


def adagrad(weights_in, accum_in, gradient):
    accum_out = accum_in + jnp.mean(gradient * gradient, axis=-1)
    weights_out = weights_in - LEARN_RATE * gradient / (jnp.sqrt(accum_out)[..., None] + EPSILON)
    return (weights_out, accum_out)


def on_device(pooled_grads, table, state, tile_mult, tile_rows):
    weights_in = table[0]
    accum_in = state[0]
    mult = tile_mult[0, 0]
    rows, width = weights_in.shape
    row_blocks = rows // mult.shape[-1]

    by_table = jnp.transpose(pooled_grads[0, 0], (1, 0, 2))
    received = lax.all_to_all(by_table, "mp", split_axis=0, concat_axis=0, tiled=True)
    partial_grad = accumulate(tile_rows[0, 0], mult, received, row_blocks)

    total_grad = sum_over_replicas(partial_grad.reshape(rows, width))

    weights_out, accum_out = adagrad(weights_in, accum_in, total_grad)
    return (weights_out[None], accum_out[None])


def solution(mesh):
    placed = (
        P("mp", "replica", None, None, None),
        P("mp", None, None),
        P("mp", None),
        P("mp", "replica", None, None, None),
        P("mp", "replica", None),
    )
    return jax.shard_map(
        on_device,
        mesh=mesh,
        in_specs=placed,
        out_specs=(P("mp", None, None), P("mp", None)),
        check_vma=False,
    )
```

```python
import jax
import jax.numpy as jnp
from jax import lax
from jax.experimental import pallas as pl
from jax.experimental.pallas import tpu as pltpu
from jax.sharding import PartitionSpec as P

LEARN_RATE = 0.5
EPSILON = 1e-06
CORES = 2
X = 4
Z = 16
HALF = Z // 2
NEAR = (1, 2, 3)
FAR = ((8, 7, 6), (5, 4))


def vmem_specs(n):
    return [pl.BlockSpec(memory_space=pltpu.VMEM)] * n


SMEM = pl.BlockSpec(memory_space=pltpu.SMEM)
PARAMS = pltpu.CompilerParams(vmem_limit_bytes=16 << 20)


def relayout(src, row_ids, local):
    samples, tables, width = local.shape
    others = (HALF - 1) * X

    def kernel(src_ref, rows_ref, in_ref, table_ref, half_ref, other_ref):
        for g in range(X):
            block = jnp.swapaxes(in_ref[:, g * Z : (g + 1) * Z, :], 0, 1)
            table_ref[g * Z : (g + 1) * Z] = block
        for j in range(X):
            half_ref[j] = table_ref[src_ref[HALF * X + j]]
        for n in range(others):
            i, j = n // X + 1, n % X
            other_ref[n] = table_ref[src_ref[(Z - i) * X + j]]
        ids = rows_ref[...].astype(jnp.float32)
        ids = jnp.concatenate([ids] * (width // ids.shape[1]), axis=1)
        other_ref[others] = jnp.broadcast_to(ids, (samples, width)).astype(other_ref.dtype)

    def out(n):
        return jax.ShapeDtypeStruct((n, samples, width), local.dtype)

    return pl.pallas_call(
        kernel,
        out_shape=[out(tables), out(X), out(others + 1)],
        in_specs=[SMEM] + vmem_specs(2),
        out_specs=vmem_specs(3),
        compiler_params=PARAMS,
        name="relayout",
    )(src, row_ids[None], local)


def regroup(src, inputs, plans):
    block = inputs[0].shape[1:]

    def kernel(src_ref, *refs):
        in_refs, out_refs = refs[: len(inputs)], refs[len(inputs) :]
        for out_ref, plan in zip(out_refs, plans):
            for n, (i, k, *place) in enumerate(plan):
                out_ref[n] = in_refs[i][src_ref[place[0]] if k is None else k]

    return pl.pallas_call(
        kernel,
        out_shape=[jax.ShapeDtypeStruct((len(p),) + block, inputs[0].dtype) for p in plans],
        in_specs=[SMEM] + vmem_specs(len(inputs)),
        out_specs=vmem_specs(len(plans)),
        compiler_params=PARAMS,
        name="regroup",
    )(src, *inputs)


def add_tiles(partial, groups, tile, mult, rows, row_blocks):
    blocks = [g for g, _ in groups]
    pairs_of = [p for _, ps in groups for p in ps]
    owner = [(n, k) for n, (_, ps) in enumerate(groups) for k in range(len(ps))]
    block, width = blocks[0].shape[1:]

    def kernel(tile_ref, rows0, rows1, mult0, mult1, *refs):
        block_refs, out_ref = refs[: len(blocks)], refs[-1]
        if partial is None:
            out_ref[...] = jnp.zeros(out_ref.shape, out_ref.dtype)
        else:
            out_ref[...] = refs[-2][...]
        for (i, j, s), (g, k) in zip(pairs_of, owner):
            t = tile_ref[i * X + j]
            mult_ref, rows_ref = (mult1, rows1) if s else (mult0, rows0)
            out_ref[rows_ref[t]] += lax.dot_general(
                mult_ref[t],
                block_refs[g][k],
                (((0,), (0,)), ((), ())),
                preferred_element_type=jnp.float32,
            )

    start = [] if partial is None else [partial]
    return pl.pallas_call(
        kernel,
        out_shape=jax.ShapeDtypeStruct((row_blocks, block, width), jnp.float32),
        in_specs=[SMEM] * 3 + vmem_specs(2 + len(blocks) + len(start)),
        out_specs=vmem_specs(1)[0],
        compiler_params=PARAMS,
        name="add_tiles",
    )(tile, *rows, *mult, *blocks, *start)


def sum_over_replicas(partial_grad):
    rows, width = partial_grad.shape
    replicas = lax.axis_size("replica")
    chips = replicas // CORES
    core = lax.axis_index("replica") % CORES
    swap = [(i, i ^ 1) for i in range(replicas)]
    same_core = [[chip * CORES + c for chip in range(chips)] for c in range(CORES)]

    chip_sum = partial_grad + lax.ppermute(partial_grad, "replica", swap)
    half = lax.dynamic_index_in_dim(
        chip_sum.reshape(CORES, rows // CORES, width), core, 0, keepdims=False
    )
    copies = jnp.broadcast_to(half[None], (chips,) + half.shape)
    shares = lax.all_to_all(
        copies, "replica", split_axis=0, concat_axis=0, axis_index_groups=same_core, tiled=True
    )
    own = jnp.sum(shares, axis=0)
    other = lax.ppermute(own, "replica", swap)
    first = core == 0
    return jnp.concatenate([jnp.where(first, own, other), jnp.where(first, other, own)])


def adagrad(weights_in, accum_in, gradient):
    accum_out = accum_in + jnp.mean(gradient * gradient, axis=-1)
    weights_out = weights_in - LEARN_RATE * gradient / (jnp.sqrt(accum_out)[..., None] + EPSILON)
    return (weights_out, accum_out)


def pairs(shift):
    replicas = 4 * CORES
    out = []
    for x in range(X):
        for z in range(Z):
            for r in range(replicas):
                c = r % CORES
                x2, z2, c2 = shift(x, z, c)
                target = ((x2 % X) * Z + z2 % Z) * replicas + r - c + c2
                out.append(((x * Z + z) * replicas + r, target))
    return out


def move(value, shift):
    return lax.ppermute(value, ("mp", "replica"), pairs(shift))


def over_z(i):
    return lambda x, z, c: (x, z + (i if c == 0 else -i), c)


def over_x(j):
    return lambda x, z, c: (x + j, z, c)


def other_core(x, z, c):
    return (x, z, 1 - c)


def exchange_and_add(local, mult, rows, row_blocks):
    mp = lax.axis_index("mp")
    x, z = mp // Z, mp % Z
    core = lax.axis_index("replica") % CORES
    way = 1 - 2 * core
    place = jnp.arange(Z * X, dtype=jnp.int32)
    shift, step = place // X, place % X
    src = (x + step) % X * Z + (z + way * shift) % Z
    tile = (x - step) % X * Z + (z - way * shift) % Z

    by_table, half, oth = relayout(src, rows, local)
    got = {HALF: move(half, over_z(HALF))}
    sib = move(oth, other_core)
    rows = (rows, sib[-1, 0, : rows.shape[0]].astype(jnp.int32))

    def both(i, j):
        return [(0, None, i * X + j), (1, (i - 1) * X + j)]

    far_shifts = (7, 6, 5, 4)
    plans = [[both(i, j)[s] for s in range(2) for j in range(X)] for i in far_shifts]
    plans += [[(0, None, j)] + [b for i in NEAR for b in both(i, j)] for j in range(X)]
    made = regroup(src, [by_table, sib], plans)
    mine, near = dict(zip(far_shifts, made)), list(made[len(far_shifts) :])
    for i in (7, 6):
        got[i] = move(mine[i], over_z(i))
    for j in range(1, X):
        near[j] = move(near[j], over_x(j))
    for i in (5, 4):
        got[i] = move(mine[i], over_z(i))
    mult = (mult, move(mult, other_core))

    def far(shifts):
        who = [(n, i, s) for n, i in enumerate(shifts) for s in range(1 if i == HALF else 2)]
        plans = [[(n, s * X + j) for n, _, s in who] for j in range(X)]
        made = list(regroup(src, [got[i] for i in shifts], plans))
        for j in range(1, X):
            made[j] = move(made[j], over_x(j))
        return [(made[j], [(i, j, s) for _, i, s in who]) for j in range(X)]

    groups = [(near[j], [(0, j, 0)]) for j in range(X)]
    groups += far(FAR[0])
    plans = [
        [(j, 1 + 2 * NEAR.index(i) + s) for s in range(2) for j in range(X)] for i in NEAR
    ]
    made = regroup(src, near, plans)
    last = []
    for i in NEAR[::-1]:
        blocks = move(made[NEAR.index(i)], over_z(i))
        last.append((blocks, [(i, j, s) for s in range(2) for j in range(X)]))
    groups += far(FAR[1])
    partial = add_tiles(None, groups, tile, mult, rows, row_blocks)
    return add_tiles(partial, last, tile, mult, rows, row_blocks)


def on_device(pooled_grads, table, state, tile_mult, tile_rows):
    weights_in = table[0]
    accum_in = state[0]
    mult = tile_mult[0, 0]
    rows, width = weights_in.shape
    row_blocks = rows // mult.shape[-1]
    partial_grad = exchange_and_add(pooled_grads[0, 0], mult, tile_rows[0, 0], row_blocks)
    total_grad = sum_over_replicas(partial_grad.reshape(rows, width))
    weights_out, accum_out = adagrad(weights_in, accum_in, total_grad)
    return (weights_out[None], accum_out[None])


def solution(mesh):
    placed = (
        P("mp", "replica", None, None, None),
        P("mp", None, None),
        P("mp", None),
        P("mp", "replica", None, None, None),
        P("mp", "replica", None),
    )
    return jax.shard_map(
        on_device,
        mesh=mesh,
        in_specs=placed,
        out_specs=(P("mp", None, None), P("mp", None)),
        check_vma=False,
    )
```

```python
import jax
import jax.numpy as jnp
from jax import lax
from jax.experimental import pallas as pl
from jax.experimental.pallas import tpu as pltpu
from jax.sharding import PartitionSpec as P

LEARN_RATE = 0.5
EPSILON = 1e-06
CORES = 2
X = 4
Z = 16
HALF = Z // 2
NEAR = (1, 2, 3, 4)
FAR = (8, 7, 6, 5)


def vmem_specs(n):
    return [pl.BlockSpec(memory_space=pltpu.VMEM)] * n


SMEM = pl.BlockSpec(memory_space=pltpu.SMEM)
PARAMS = pltpu.CompilerParams(vmem_limit_bytes=16 << 20)


def in_hbm(value):
    return pltpu.with_memory_space_constraint(value, pltpu.HBM)


def relayout(src, row_ids, local):
    samples, tables, width = local.shape
    others = (HALF - 1) * X

    def kernel(src_ref, rows_hbm, in_hbm, table_ref, half_ref, other_ref, rows_ref, in_ref, sems):
        copies = [pltpu.make_async_copy(rows_hbm, rows_ref, sems.at[X])]
        for g in range(X):
            part = in_hbm.at[:, g * Z : (g + 1) * Z, :]
            copies.append(pltpu.make_async_copy(part, in_ref.at[g], sems.at[g]))
        for copy in copies:
            copy.start()
        copies[0].wait()
        for g in range(X):
            copies[1 + g].wait()
            table_ref[g * Z : (g + 1) * Z] = jnp.swapaxes(in_ref[g], 0, 1)
        for j in range(X):
            half_ref[j] = table_ref[src_ref[HALF * X + j]]
        for n in range(others):
            i, j = n // X + 1, n % X
            other_ref[n] = table_ref[src_ref[(Z - i) * X + j]]
        ids = rows_ref[...].astype(jnp.float32)
        ids = jnp.concatenate([ids] * (width // ids.shape[1]), axis=1)
        other_ref[others] = jnp.broadcast_to(ids, (samples, width)).astype(other_ref.dtype)

    def out(n):
        return jax.ShapeDtypeStruct((n, samples, width), local.dtype)

    return pl.pallas_call(
        kernel,
        out_shape=[out(tables), out(X), out(others + 1)],
        in_specs=[SMEM] + [pl.BlockSpec(memory_space=pltpu.HBM)] * 2,
        out_specs=vmem_specs(3),
        scratch_shapes=[
            pltpu.VMEM((1, row_ids.shape[0]), row_ids.dtype),
            pltpu.VMEM((X, samples, Z, width), local.dtype),
            pltpu.SemaphoreType.DMA((X + 1,)),
        ],
        compiler_params=PARAMS,
        name="relayout",
    )(src, in_hbm(row_ids[None]), in_hbm(local))


def regroup(src, inputs, plans, after=()):
    block = inputs[0].shape[1:]

    def kernel(src_ref, *refs):
        in_refs, out_refs = refs[: len(inputs)], refs[len(inputs) + len(after) :]
        for out_ref, plan in zip(out_refs, plans):
            for n, (i, k, *place) in enumerate(plan):
                out_ref[n] = in_refs[i][src_ref[place[0]] if k is None else k]

    return pl.pallas_call(
        kernel,
        out_shape=[jax.ShapeDtypeStruct((len(p),) + block, inputs[0].dtype) for p in plans],
        in_specs=[SMEM] + vmem_specs(len(inputs)) + [pl.BlockSpec(memory_space=pl.ANY)] * len(after),
        out_specs=vmem_specs(len(plans)),
        compiler_params=PARAMS,
        name="regroup",
    )(src, *inputs, *after)


def add_tiles(partial, groups, tile, mult, rows, row_blocks):
    blocks = [g for g, _ in groups]
    pairs_of = [p for _, ps in groups for p in ps]
    owner = [(n, k) for n, (_, ps) in enumerate(groups) for k in range(len(ps))]
    block, width = blocks[0].shape[1:]

    def kernel(tile_ref, rows0, rows1, mult0, mult1, *refs):
        block_refs, out_ref = refs[: len(blocks)], refs[-1]
        if partial is None:
            out_ref[...] = jnp.zeros(out_ref.shape, out_ref.dtype)
        else:
            out_ref[...] = refs[-2][...]
        for (i, j, s), (g, k) in zip(pairs_of, owner):
            t = tile_ref[i * X + j]
            mult_ref, rows_ref = (mult1, rows1) if s else (mult0, rows0)
            out_ref[rows_ref[t]] += lax.dot_general(
                mult_ref[t],
                block_refs[g][k],
                (((0,), (0,)), ((), ())),
                preferred_element_type=jnp.float32,
            )

    start = [] if partial is None else [partial]
    return pl.pallas_call(
        kernel,
        out_shape=jax.ShapeDtypeStruct((row_blocks, block, width), jnp.float32),
        in_specs=[SMEM] * 3 + vmem_specs(2 + len(blocks) + len(start)),
        out_specs=vmem_specs(1)[0],
        compiler_params=PARAMS,
        name="add_tiles",
    )(tile, *rows, *mult, *blocks, *start)


def sum_over_replicas(partial_grad):
    rows, width = partial_grad.shape
    replicas = lax.axis_size("replica")
    chips = replicas // CORES
    core = lax.axis_index("replica") % CORES
    swap = [(i, i ^ 1) for i in range(replicas)]
    same_core = [[chip * CORES + c for chip in range(chips)] for c in range(CORES)]

    chip_sum = partial_grad + lax.ppermute(partial_grad, "replica", swap)
    half = lax.dynamic_index_in_dim(
        chip_sum.reshape(CORES, rows // CORES, width), core, 0, keepdims=False
    )
    copies = jnp.broadcast_to(half[None], (chips,) + half.shape)
    shares = lax.all_to_all(
        copies, "replica", split_axis=0, concat_axis=0, axis_index_groups=same_core, tiled=True
    )
    own = jnp.sum(shares, axis=0)
    other = lax.ppermute(own, "replica", swap)
    first = core == 0
    return jnp.concatenate([jnp.where(first, own, other), jnp.where(first, other, own)])


def adagrad(weights_in, accum_in, gradient):
    accum_out = accum_in + jnp.mean(gradient * gradient, axis=-1)
    weights_out = weights_in - LEARN_RATE * gradient / (jnp.sqrt(accum_out)[..., None] + EPSILON)
    return (weights_out, accum_out)


def pairs(shift):
    replicas = 4 * CORES
    out = []
    for x in range(X):
        for z in range(Z):
            for r in range(replicas):
                c = r % CORES
                x2, z2, c2 = shift(x, z, c)
                target = ((x2 % X) * Z + z2 % Z) * replicas + r - c + c2
                out.append(((x * Z + z) * replicas + r, target))
    return out


def move(value, shift):
    return lax.ppermute(value, ("mp", "replica"), pairs(shift))


def over_z(i):
    return lambda x, z, c: (x, z + (i if c == 0 else -i), c)


def over_x(j):
    return lambda x, z, c: (x + j, z, c)


def other_core(x, z, c):
    return (x, z, 1 - c)


def exchange_and_add(local, mult, rows, row_blocks):
    mp = lax.axis_index("mp")
    x, z = mp // Z, mp % Z
    core = lax.axis_index("replica") % CORES
    way = 1 - 2 * core
    place = jnp.arange(Z * X, dtype=jnp.int32)
    shift, step = place // X, place % X
    src = (x + step) % X * Z + (z + way * shift) % Z
    tile = (x - step) % X * Z + (z - way * shift) % Z

    by_table, half, oth = relayout(src, rows, local)
    got = {HALF: move(half, over_z(HALF))}
    sib = move(oth, other_core)
    rows = (rows, sib[-1, 0, : rows.shape[0]].astype(jnp.int32))

    def both(i, j):
        return [(0, None, i * X + j), (1, (i - 1) * X + j)]

    far_shifts = FAR[1:]
    plans = [[both(i, j)[s] for s in range(2) for j in range(X)] for i in far_shifts]
    plans += [[(0, None, j)] + [b for i in NEAR for b in both(i, j)] for j in range(X)]
    made = regroup(src, [by_table, sib], plans)
    mine, near = dict(zip(far_shifts, made)), list(made[len(far_shifts) :])
    for i in far_shifts:
        got[i] = move(mine[i], over_z(i))
    for j in range(1, X):
        near[j] = move(near[j], over_x(j))
    mult = (mult, move(mult, other_core))

    def far(shifts):
        who = [(n, i, s) for n, i in enumerate(shifts) for s in range(1 if i == HALF else 2)]
        plans = [[(n, s * X + j) for n, _, s in who] for j in range(X)]
        made = list(regroup(src, [got[i] for i in shifts], plans, mult[1:]))
        for j in range(1, X):
            made[j] = move(made[j], over_x(j))
        return [(made[j], [(i, j, s) for _, i, s in who]) for j in range(X)]

    groups = [(near[j], [(0, j, 0)]) for j in range(X)]
    groups += far(FAR)
    plans = [
        [(j, 1 + 2 * NEAR.index(i) + s) for s in range(2) for j in range(X)] for i in NEAR
    ]
    made = regroup(src, near, plans)
    last = []
    for i in NEAR[::-1]:
        blocks = move(made[NEAR.index(i)], over_z(i))
        last.append((blocks, [(i, j, s) for s in range(2) for j in range(X)]))
    partial = add_tiles(None, groups, tile, mult, rows, row_blocks)
    return add_tiles(partial, last, tile, mult, rows, row_blocks)


def on_device(pooled_grads, table, state, tile_mult, tile_rows):
    weights_in = table[0]
    accum_in = state[0]
    mult = tile_mult[0, 0]
    rows, width = weights_in.shape
    row_blocks = rows // mult.shape[-1]
    partial_grad = exchange_and_add(pooled_grads[0, 0], mult, tile_rows[0, 0], row_blocks)
    total_grad = sum_over_replicas(partial_grad.reshape(rows, width))
    weights_out, accum_out = adagrad(weights_in, accum_in, total_grad)
    return (weights_out[None], accum_out[None])


def solution(mesh):
    placed = (
        P("mp", "replica", None, None, None),
        P("mp", None, None),
        P("mp", None),
        P("mp", "replica", None, None, None),
        P("mp", "replica", None),
    )
    return jax.shard_map(
        on_device,
        mesh=mesh,
        in_specs=placed,
        out_specs=(P("mp", None, None), P("mp", None)),
        check_vma=False,
    )
```

```python
import jax
import jax.numpy as jnp
from jax import lax
from jax.experimental import pallas as pl
from jax.experimental.pallas import tpu as pltpu
from jax.sharding import PartitionSpec as P

LEARN_RATE = 0.5
EPSILON = 1e-06
CORES = 2
X = 4
Z = 16
HALF = Z // 2
NEAR = (1, 2, 3, 4)
FAR = (8, 7, 6, 5)


def vmem_specs(n):
    return [pl.BlockSpec(memory_space=pltpu.VMEM)] * n


SMEM = pl.BlockSpec(memory_space=pltpu.SMEM)
PARAMS = pltpu.CompilerParams(vmem_limit_bytes=16 << 20)


def in_hbm(value):
    return pltpu.with_memory_space_constraint(value, pltpu.HBM)


def relayout(src, row_ids, local):
    samples, tables, width = local.shape
    others = (HALF - 1) * X

    def kernel(src_ref, rows_hbm, in_hbm, table_ref, half_ref, other_ref, rows_ref, in_ref, sems):
        copies = [pltpu.make_async_copy(rows_hbm, rows_ref, sems.at[X])]
        for g in range(X):
            part = in_hbm.at[:, g * Z : (g + 1) * Z, :]
            copies.append(pltpu.make_async_copy(part, in_ref.at[g], sems.at[g]))
        for copy in copies:
            copy.start()
        copies[0].wait()
        for g in range(X):
            copies[1 + g].wait()
            table_ref[g * Z : (g + 1) * Z] = jnp.swapaxes(in_ref[g], 0, 1)
        for j in range(X):
            half_ref[j] = table_ref[src_ref[HALF * X + j]]
        for n in range(others):
            i, j = n // X + 1, n % X
            other_ref[n] = table_ref[src_ref[(Z - i) * X + j]]
        ids = rows_ref[...].astype(jnp.float32)
        ids = jnp.concatenate([ids] * (width // ids.shape[1]), axis=1)
        other_ref[others] = jnp.broadcast_to(ids, (samples, width)).astype(other_ref.dtype)

    def out(n):
        return jax.ShapeDtypeStruct((n, samples, width), local.dtype)

    return pl.pallas_call(
        kernel,
        out_shape=[out(tables), out(X), out(others + 1)],
        in_specs=[SMEM] + [pl.BlockSpec(memory_space=pltpu.HBM)] * 2,
        out_specs=vmem_specs(3),
        scratch_shapes=[
            pltpu.VMEM((1, row_ids.shape[0]), row_ids.dtype),
            pltpu.VMEM((X, samples, Z, width), local.dtype),
            pltpu.SemaphoreType.DMA((X + 1,)),
        ],
        compiler_params=PARAMS,
        name="relayout",
    )(src, in_hbm(row_ids[None]), in_hbm(local))


def regroup(src, inputs, plans, after=()):
    block = inputs[0].shape[1:]

    def kernel(src_ref, *refs):
        in_refs, out_refs = refs[: len(inputs)], refs[len(inputs) + len(after) :]
        for out_ref, plan in zip(out_refs, plans):
            for n, (i, k, *place) in enumerate(plan):
                out_ref[n] = in_refs[i][src_ref[place[0]] if k is None else k]

    return pl.pallas_call(
        kernel,
        out_shape=[jax.ShapeDtypeStruct((len(p),) + block, inputs[0].dtype) for p in plans],
        in_specs=[SMEM] + vmem_specs(len(inputs)) + [pl.BlockSpec(memory_space=pl.ANY)] * len(after),
        out_specs=vmem_specs(len(plans)),
        compiler_params=PARAMS,
        name="regroup",
    )(src, *inputs, *after)


def add_tiles(partial, groups, ids, mult, row_blocks):
    blocks = [g for g, _ in groups]
    pairs_of = [p for _, ps in groups for p in ps]
    owner = [(n, k) for n, (_, ps) in enumerate(groups) for k in range(len(ps))]
    block, width = blocks[0].shape[1:]

    def kernel(ids_ref, mult0, mult1, *refs):
        block_refs, out_ref = refs[: len(blocks)], refs[-1]
        if partial is None:
            out_ref[...] = jnp.zeros(out_ref.shape, out_ref.dtype)
        else:
            out_ref[...] = refs[-2][...]
        for (i, j, s), (g, k) in zip(pairs_of, owner):
            t = ids_ref[i * X + j]
            mult_ref = mult1 if s else mult0
            out_ref[ids_ref[(1 + s) * X * Z + t]] += lax.dot_general(
                mult_ref[t],
                block_refs[g][k],
                (((0,), (0,)), ((), ())),
                preferred_element_type=jnp.float32,
            )

    start = [] if partial is None else [partial]
    return pl.pallas_call(
        kernel,
        out_shape=jax.ShapeDtypeStruct((row_blocks, block, width), jnp.float32),
        in_specs=[SMEM] + vmem_specs(2 + len(blocks) + len(start)),
        out_specs=vmem_specs(1)[0],
        compiler_params=PARAMS,
        name="add_tiles",
    )(ids, *mult, *blocks, *start)


def sum_over_replicas(partial_grad):
    rows, width = partial_grad.shape
    replicas = lax.axis_size("replica")
    chips = replicas // CORES
    core = lax.axis_index("replica") % CORES
    swap = [(i, i ^ 1) for i in range(replicas)]
    same_core = [[chip * CORES + c for chip in range(chips)] for c in range(CORES)]

    chip_sum = partial_grad + lax.ppermute(partial_grad, "replica", swap)
    half = lax.dynamic_index_in_dim(
        chip_sum.reshape(CORES, rows // CORES, width), core, 0, keepdims=False
    )
    copies = jnp.broadcast_to(half[None], (chips,) + half.shape)
    shares = lax.all_to_all(
        copies, "replica", split_axis=0, concat_axis=0, axis_index_groups=same_core, tiled=True
    )
    own = jnp.sum(shares, axis=0)
    other = lax.ppermute(own, "replica", swap)
    return core, own, other


def update(core, own, other, weights_in, accum_in):
    rows, width = weights_in.shape
    half = rows // CORES

    def kernel(core_ref, own_ref, other_ref, weights_ref, accum_ref, weights_out, accum_out):
        first = core_ref[0] == 0
        for at in range(0, rows, width):
            part = slice(at % half, at % half + width)
            one, two = own_ref[part], other_ref[part]
            grad = jnp.where(first, one, two) if at < half else jnp.where(first, two, one)
            square = jnp.mean(grad * grad, axis=-1, keepdims=True)
            before = jnp.broadcast_to(accum_ref[:, at : at + width], (width, width)).T
            accum = before + square
            rate = LEARN_RATE * grad / (jnp.sqrt(accum) + EPSILON)
            weights_out[at : at + width] = weights_ref[at : at + width] - rate
            accum_out[:, at : at + width] = accum.T[:1]

    return pl.pallas_call(
        kernel,
        out_shape=[
            jax.ShapeDtypeStruct(weights_in.shape, weights_in.dtype),
            jax.ShapeDtypeStruct(accum_in.shape, accum_in.dtype),
        ],
        in_specs=[SMEM] + vmem_specs(4),
        out_specs=vmem_specs(2),
        compiler_params=PARAMS,
        name="update",
    )(core[None], own, other, weights_in, accum_in)


def pairs(shift):
    replicas = 4 * CORES
    out = []
    for x in range(X):
        for z in range(Z):
            for r in range(replicas):
                c = r % CORES
                x2, z2, c2 = shift(x, z, c)
                target = ((x2 % X) * Z + z2 % Z) * replicas + r - c + c2
                out.append(((x * Z + z) * replicas + r, target))
    return out


def move(value, shift):
    return lax.ppermute(value, ("mp", "replica"), pairs(shift))


def over_z(i):
    return lambda x, z, c: (x, z + (i if c == 0 else -i), c)


def over_x(j):
    return lambda x, z, c: (x + j, z, c)


def other_core(x, z, c):
    return (x, z, 1 - c)


def exchange_and_add(local, mult, rows, row_blocks):
    mp = lax.axis_index("mp")
    x, z = mp // Z, mp % Z
    core = lax.axis_index("replica") % CORES
    way = 1 - 2 * core
    place = jnp.arange(Z * X, dtype=jnp.int32)
    shift, step = place // X, place % X
    src = (x + step) % X * Z + (z + way * shift) % Z
    tile = (x - step) % X * Z + (z - way * shift) % Z

    by_table, half, oth = relayout(src, rows, local)
    got = {HALF: move(half, over_z(HALF))}
    sib = move(oth, other_core)
    ids = jnp.concatenate([tile, rows, sib[-1, 0, : rows.shape[0]].astype(jnp.int32)])

    def both(i, j):
        return [(0, None, i * X + j), (1, (i - 1) * X + j)]

    far_shifts = FAR[1:]
    plans = [[both(i, j)[s] for s in range(2) for j in range(X)] for i in far_shifts]
    plans += [[(0, None, j)] + [b for i in NEAR for b in both(i, j)] for j in range(X)]
    made = regroup(src, [by_table, sib], plans)
    mine, near = dict(zip(far_shifts, made)), list(made[len(far_shifts) :])
    for i in far_shifts:
        got[i] = move(mine[i], over_z(i))
    for j in range(1, X):
        near[j] = move(near[j], over_x(j))
    mult = (mult, move(mult, other_core))

    def far(shifts):
        who = [(n, i, s) for n, i in enumerate(shifts) for s in range(1 if i == HALF else 2)]
        plans = [[(n, s * X + j) for n, _, s in who] for j in range(X)]
        made = list(regroup(src, [got[i] for i in shifts], plans, mult[1:]))
        for j in range(1, X):
            made[j] = move(made[j], over_x(j))
        return [(made[j], [(i, j, s) for _, i, s in who]) for j in range(X)]

    groups = [(near[j], [(0, j, 0)]) for j in range(X)]
    groups += far(FAR)
    plans = [
        [(j, 1 + 2 * NEAR.index(i) + s) for s in range(2) for j in range(X)] for i in NEAR
    ]
    made = regroup(src, near, plans)
    last = []
    for i in NEAR[::-1]:
        blocks = move(made[NEAR.index(i)], over_z(i))
        last.append((blocks, [(i, j, s) for s in range(2) for j in range(X)]))
    partial = add_tiles(None, groups, ids, mult, row_blocks)
    return add_tiles(partial, last, ids, mult, row_blocks)


def on_device(pooled_grads, table, state, tile_mult, tile_rows):
    weights_in = table[0]
    mult = tile_mult[0, 0]
    rows, width = weights_in.shape
    row_blocks = rows // mult.shape[-1]
    partial_grad = exchange_and_add(pooled_grads[0, 0], mult, tile_rows[0, 0], row_blocks)
    core, own, other = sum_over_replicas(partial_grad.reshape(rows, width))
    weights_out, accum_out = update(core, own, other, weights_in, state)
    return (weights_out[None], accum_out)


def solution(mesh):
    placed = (
        P("mp", "replica", None, None, None),
        P("mp", None, None),
        P("mp", None),
        P("mp", "replica", None, None, None),
        P("mp", "replica", None),
    )
    return jax.shard_map(
        on_device,
        mesh=mesh,
        in_specs=placed,
        out_specs=(P("mp", None, None), P("mp", None)),
        check_vma=False,
    )
```
